32 devices in a mesh: sta: 8 (over z, x), seg: 4 (over y, core).
Axes of the slice: x: 2, y: 2, z: 4, core: 2. Of those that a mesh axis runs over, the one named last changes fastest.
Arguments:
- traces: float32 [128, 8, 4096], P('sta', 'seg'), may hold values from -60 to 60, as said below
- pair_blocks: int32 [256, 2], P('sta'), may hold values from 0 to 31, as said below
- pair_counts: int32 [8], P('sta'), may hold values from 4 to 32, as said below
Outputs:
- correlations: bfloat16 [256, 4, 4, 4096], P(('sta', 'seg'))
The draws below stay inside these ranges and needn't reach their ends.
Inputs may be any that keep to these rules, and one draw needn't show every extreme that they name: `traces`: random scales per station. `pair_blocks`: rows k * 32 to (k + 1) * 32 - 1 belong to owner k: their first block is one of owner k's stations' blocks, numbers k * 4 to (k + 1) * 4 - 1. Over the 32 rows of one owner, at most 8 second blocks lie in the blocks of any one index of sta, and every owner has exactly 8 for some index. `pair_counts`: one owner has exactly 32 live slots; live slots are the first ones of an owner.
All inputs are finite; a program needn't handle non-finite values.
Results may differ from the reference program's by a relative error of at most 0.0057.
Values may be sent and summed in bfloat16 or wider, within the bound.
No kernel may reach another device: no remote copies, remote signals or barrier semaphores. Data moves between devices by JAX's collectives and lax.ppermute only.
A program may use at most 128 MiB of HBM per device.

```python
import math
import jax
import jax.numpy as jnp
from jax import lax

L = 4096
F = 2048
BLK = 4
SEGS = 8
S_DEV = 16
PAIR_DEV = 32
STATIONS = 128
BLOCKS = 32
SLOTS = 256
CAP = 8
N_STA = 8


def draw_traces(key, part):
    key_scale, key_noise = jax.random.split(key, 2)
    log_scale = jax.random.uniform(key_scale, (STATIONS, 1, 1), jnp.float32, 0.0, math.log(10.0))
    station_scale = jnp.exp(log_scale)
    noise_part = jnp.clip(jax.random.normal(key_noise, (STATIONS, SEGS, L), jnp.float32), -6.0, 6.0)
    return (station_scale * noise_part).astype(jnp.float32)


def draw_pair_blocks(key, part):
    block_count = S_DEV // BLK

    def one_owner(owner):
        owner_key = jax.random.fold_in(key, owner)
        key_perm, key_order, key_first, key_second = jax.random.split(owner_key, 4)
        shuffled = jax.random.permutation(key_perm, CAP * N_STA)
        homes = shuffled // CAP
        leading_home = homes[0]
        scores = jnp.where(homes == leading_home, -1, jnp.arange(CAP * N_STA))
        ordering = jnp.argsort(scores, stable=True)
        chosen = homes[ordering][:PAIR_DEV]
        chosen = jax.random.permutation(key_order, chosen)
        local_first = jax.random.randint(key_first, (PAIR_DEV,), 0, block_count)
        local_second = jax.random.randint(key_second, (PAIR_DEV,), 0, block_count)
        return jnp.stack([owner * block_count + local_first, chosen * block_count + local_second], axis=1)
    result = jax.vmap(one_owner)(jnp.arange(N_STA))
    return result.reshape(N_STA * PAIR_DEV, 2).astype(jnp.int32)


def draw_pair_counts(key, part):
    key_counts, key_full = jax.random.split(jax.random.fold_in(key, 7), 2)
    counts = jax.random.randint(key_counts, (N_STA,), PAIR_DEV // 8, 3 * PAIR_DEV // 4 + 1)
    full_owner = jax.random.randint(key_full, (), 0, N_STA)
    return jnp.where(jnp.arange(N_STA) == full_owner, PAIR_DEV, counts).astype(jnp.int32)


def setup_inputs(seed: int = 0) -> dict:
    streams_of = jax.random.split(jax.random.key(seed), 4)
    traces = draw_traces(jax.random.fold_in(streams_of[3], 71), 0)
    pair_blocks = draw_pair_blocks(jax.random.fold_in(streams_of[3], 71), 0)
    pair_counts = draw_pair_counts(jax.random.fold_in(streams_of[3], 71), 0)
    return dict(traces=traces, pair_blocks=pair_blocks, pair_counts=pair_counts)


band_count = 32
epsilon = 1e-06

def whitened(traces):
    centred = traces - lax.optimization_barrier(jnp.mean(traces, axis=-1, keepdims=True))
    spectrum = jnp.fft.rfft(centred, axis=-1)[..., :L // 2]
    real_part = jnp.real(spectrum)
    imag_part = jnp.imag(spectrum)
    leading = traces.shape[:-1]
    band_power = (real_part * real_part + imag_part * imag_part).reshape(leading + (band_count, -1))
    inverse_amp = 1.0 / jnp.sqrt(lax.optimization_barrier(jnp.mean(band_power, axis=-1, keepdims=True)) + epsilon)
    white_real = (real_part.reshape(leading + (band_count, -1)) * inverse_amp).reshape(leading + (-1,))
    white_imag = (imag_part.reshape(leading + (band_count, -1)) * inverse_amp).reshape(leading + (-1,))
    return (white_real.astype(jnp.bfloat16), white_imag.astype(jnp.bfloat16))

def reference(traces, pair_blocks, pair_counts):
    white_real, white_imag = whitened(traces)
    block_real = white_real.reshape(BLOCKS, BLK, SEGS, F)
    block_imag = white_imag.reshape(BLOCKS, BLK, SEGS, F)
    owner_pairs = pair_blocks.reshape(N_STA, PAIR_DEV, 2)
    highest = lax.Precision.HIGHEST

    def contract(one_side, other_side):
        return jnp.einsum('pisf,pjsf->pijf', one_side, other_side, precision=highest)

    def per_owner(packed):
        slot_pairs, live_count = packed
        first_real = block_real[slot_pairs[:, 0]].astype(jnp.float32)
        first_imag = block_imag[slot_pairs[:, 0]].astype(jnp.float32)
        second_real = block_real[slot_pairs[:, 1]].astype(jnp.float32)
        second_imag = block_imag[slot_pairs[:, 1]].astype(jnp.float32)
        cross_real = contract(first_real, second_real) + contract(first_imag, second_imag)
        cross_imag = contract(first_imag, second_real) - contract(first_real, second_imag)
        live_mask = (jnp.arange(PAIR_DEV) < live_count).astype(jnp.float32)[:, None, None, None]
        cross_spec = (cross_real + 1j * cross_imag) * live_mask
        padded = jnp.concatenate([cross_spec, jnp.zeros(cross_spec.shape[:-1] + (1,), cross_spec.dtype)], axis=-1)
        series = jnp.fft.irfft(padded, n=L, axis=-1) * (L / math.sqrt(F * SEGS))
        return series.astype(jnp.bfloat16)
    stacked = lax.map(per_owner, (owner_pairs, pair_counts))
    return stacked.reshape(SLOTS, BLK, BLK, L)
```

```python
import math

import jax
import jax.numpy as jnp
import numpy as np
from jax import lax
from jax.experimental import pallas as pl
from jax.experimental.pallas import tpu as pltpu
from jax.sharding import PartitionSpec as P

BLK = 4
SEGS = 8
BANDS = 32
EPSILON = 1e-06
OUTER = 16
LANES = 128
HALF = LANES // 2
HIGHEST = lax.Precision.HIGHEST


def times_root(value, numerator, period):
    re, im = value
    eighth = (8 * numerator) % (8 * period)
    if eighth % period == 0:
        step = eighth // period
        if step == 0:
            return value
        if step == 2:
            return (None if im is None else -im, re)
        if step == 4:
            return (-re, None if im is None else -im)
        if step == 6:
            return (im, -re)
    cos = math.cos(2.0 * math.pi * numerator / period)
    sin = math.sin(2.0 * math.pi * numerator / period)
    if im is None:
        return (re * cos, re * sin)
    if re is None:
        return (im * -sin, im * cos)
    return (re * cos - im * sin, re * sin + im * cos)


def plus(one, two):
    parts = []
    for left, right in zip(one, two):
        parts.append(right if left is None else left if right is None else left + right)
    return tuple(parts)


def minus(one, two):
    parts = []
    for left, right in zip(one, two):
        if right is None:
            parts.append(left)
        elif left is None:
            parts.append(-right)
        else:
            parts.append(left - right)
    return tuple(parts)


def conj(value):
    return (value[0], None if value[1] is None else -value[1])


def real_dft(samples):
    count = len(samples)
    if count == 1:
        return [(samples[0], None)]
    if count == 2:
        return [(samples[0] + samples[1], None), (samples[0] - samples[1], None)]
    even, odd = real_dft(samples[0::2]), real_dft(samples[1::2])
    result = [None] * (count // 2 + 1)
    for k in range(count // 4 + 1):
        turned = times_root(odd[k], -k, count)
        result[k] = plus(even[k], turned)
        result[count // 2 - k] = conj(minus(even[k], turned))
    return result


def real_inverse(count, spectrum):
    if count == 2:
        return [spectrum[0][0] + spectrum[1][0], spectrum[0][0] - spectrum[1][0]]
    half = count // 2
    even, odd = [], []
    for k in range(half // 2 + 1):
        mirror = conj(spectrum[half - k])
        even.append(plus(spectrum[k], mirror))
        odd.append(times_root(minus(spectrum[k], mirror), k, count))
    for part in (even, odd):
        part[0] = (part[0][0], None)
        part[-1] = (part[-1][0], None)
    out = [None] * count
    out[0::2] = real_inverse(half, even)
    out[1::2] = real_inverse(half, odd)
    return out


def lane_bins():
    lane = np.arange(2 * LANES)
    chunk, inside = lane // LANES, lane % LANES
    return inside // HALF, chunk * HALF + inside % HALF


def forward_tables(length):
    inner = length // OUTER
    part, q = lane_bins()
    b = np.arange(inner)
    angle = 2.0 * np.pi * ((b[:, None] * q[None, :]) % inner) / inner
    cos, sin = np.cos(angle), np.sin(angle)
    from_re = np.where(part == 0, cos, -sin)
    from_im = np.where(part == 0, sin, cos)
    matrix = np.concatenate([from_re, from_im], axis=0).astype(np.float32)
    k = np.arange(OUTER)
    turn = -2.0 * np.pi * (k[:, None] * b[None, :]) / length
    twist = np.stack([np.cos(turn), np.sin(turn)]).astype(np.float32)
    per_band = length // 2 // BANDS
    band = q * OUTER // per_band
    bands = (band[:, None] == band[None, :]).astype(np.float32)
    return matrix, twist, bands, per_band


def inverse_tables(length):
    inner = length // OUTER
    part, q = lane_bins()
    v = np.arange(inner)
    angle = 2.0 * np.pi * ((q[:, None] * v[None, :]) % inner) / inner
    cos, sin = np.cos(angle), np.sin(angle)
    part = part[:, None]
    to_re = np.where(part == 0, cos, -sin)
    to_im = np.where(part == 0, sin, cos)
    matrix = np.concatenate([to_re, to_im], axis=1).astype(jnp.bfloat16)
    k = np.arange(OUTER)
    turn = 2.0 * np.pi * (k[:, None] * v[None, :]) / length
    scale = 2.0 / math.sqrt(length // 2 * SEGS)
    twist = (scale * np.stack([np.cos(turn), np.sin(turn)])).astype(np.float32)
    return matrix, twist


def whiten_kernel(group_count, per_band, me_ref, x_ref, mat_ref, twist_ref, band_ref, *refs):
    outs, (z_ref, spec_ref, rows_ref) = refs[:-3], refs[-3:]
    rows, length = x_ref.shape
    inner = length // OUTER
    group = OUTER // group_count
    mean = jnp.sum(x_ref[...], axis=1, keepdims=True) * (1.0 / length)
    samples = [x_ref[:, a * inner : (a + 1) * inner] - mean for a in range(OUTER)]
    half = real_dft(samples)
    for k in range(OUTER):
        re, im = half[k] if k <= OUTER // 2 else conj(half[OUTER - k])
        cos, sin = twist_ref[0, k : k + 1, :], twist_ref[1, k : k + 1, :]
        if im is None:
            z_re, z_im = re * cos, re * sin
        else:
            z_re, z_im = re * cos - im * sin, re * sin + im * cos
        z_ref[k * rows : (k + 1) * rows, 0:inner] = z_re
        z_ref[k * rows : (k + 1) * rows, inner:] = z_im
    tile = 4 * rows

    def transform(step, power):
        at = pl.multiple_of(step * tile, tile)
        spec = jnp.dot(
            z_ref[pl.ds(at, tile), :], mat_ref[...], precision=HIGHEST, preferred_element_type=jnp.float32
        )
        spec_ref[pl.ds(at, tile), :] = spec
        square = spec * spec
        return power + sum(square[j * rows : (j + 1) * rows] for j in range(4))

    power = lax.fori_loop(0, OUTER // 4, transform, jnp.zeros((rows, 2 * LANES), jnp.float32))
    mean_power = jnp.dot(power, band_ref[...], precision=HIGHEST, preferred_element_type=jnp.float32)
    inverse_amp = 1.0 / jnp.sqrt(mean_power * (1.0 / per_band) + EPSILON)
    me = me_ref[0]
    for d in range(group_count):
        first = lax.bitwise_xor(me, d) * group
        for kk in range(group):
            at = pl.multiple_of((first + kk) * rows, rows)
            white = spec_ref[pl.ds(at, rows), :] * inverse_amp
            rows_ref[0, pl.ds(kk, rows, stride=group), :] = white[:, :LANES]
            rows_ref[1, pl.ds(kk, rows, stride=group), :] = white[:, LANES:]
        for chunk in range(2):
            outs[chunk * group_count + d][...] = rows_ref[chunk].astype(jnp.bfloat16)


def whiten(me, traces, group_count):
    stations, seg_here, length = traces.shape
    rows = stations * seg_here
    matrix, twist, bands, per_band = forward_tables(length)
    out_rows = rows * OUTER // group_count
    vmem = pl.BlockSpec(memory_space=pltpu.VMEM)
    flat = pl.pallas_call(
        lambda *refs: whiten_kernel(group_count, per_band, *refs),
        out_shape=[jax.ShapeDtypeStruct((out_rows, LANES), jnp.bfloat16)] * (2 * group_count),
        in_specs=[pl.BlockSpec(memory_space=pltpu.SMEM)] + [vmem] * 4,
        out_specs=[vmem] * (2 * group_count),
        scratch_shapes=[
            pltpu.VMEM((OUTER * rows, 2 * length // OUTER), jnp.float32),
            pltpu.VMEM((OUTER * rows, 2 * LANES), jnp.float32),
            pltpu.VMEM((2, out_rows, LANES), jnp.float32),
        ],
        name="whiten",
    )(me, traces.reshape(rows, length), matrix, twist, bands)
    return [flat[:group_count], flat[group_count:]]


def cross_kernel(group_count, piece_count, chunk, scalar_ref, *refs):
    pieces = refs[:piece_count]
    outs = refs[piece_count : piece_count + group_count]
    held, sems = refs[-2:]
    copies = []
    if piece_count == 1:
        copies.append(pltpu.make_async_copy(pieces[0], held, sems.at[0]))
    else:
        for r in range(piece_count):
            copies.append(pltpu.make_async_copy(pieces[r], held.at[r], sems.at[r]))
    for copy in copies:
        copy.start()
    for copy in copies:
        copy.wait()
    me, count, own = scalar_ref[3, 0], scalar_ref[3, 1], scalar_ref[3, 2]
    lane = lax.broadcasted_iota(jnp.int32, (8, LANES), 1)
    sub = lax.broadcasted_iota(jnp.int32, (8, LANES), 0)
    low_lane = lane < HALF
    low_sub = sub < 4
    sign = jnp.where(low_lane, 1.0, -1.0).astype(jnp.float32)
    weight = jnp.ones((8, LANES), jnp.float32)
    if chunk == 0:
        zero_bin = (lane % HALF == 0) & (sub % 4 == 0) & (me == 0)
        weight = jnp.where(zero_bin, 0.5, 1.0).astype(jnp.float32)
    sign_weight = sign
    block_rows = 8 * BLK
    slots_each = outs[0].shape[0] // (BLK * BLK * 4)
    for d in range(group_count):
        out = outs[d]
        base = lax.bitwise_xor(me, d) * slots_each

        def one_slot(i, carry, out=out, base=base):
            p = base + i
            at = pl.multiple_of(i * (BLK * BLK * 4), BLK * BLK * 4)

            @pl.when(p < count)
            def _():
                first = pl.multiple_of(scalar_ref[0, p] * block_rows, block_rows)
                piece = scalar_ref[1, p]
                second = pl.multiple_of(scalar_ref[2, p] * block_rows, block_rows)
                direct = [[None] * BLK for _ in range(BLK)]
                crossed = [[None] * BLK for _ in range(BLK)]
                for g in range(group_count):
                    one = held[own, g, pl.ds(first, block_rows), :].astype(jnp.float32)
                    two = held[piece, g, pl.ds(second, block_rows), :].astype(jnp.float32)
                    swapped = pltpu.roll(two, HALF, 1)
                    for a in range(BLK):
                        left = one[8 * a : 8 * a + 8]
                        for b in range(BLK):
                            straight = left * two[8 * b : 8 * b + 8]
                            across = left * swapped[8 * b : 8 * b + 8]
                            if g == 0:
                                direct[a][b], crossed[a][b] = straight, across
                            else:
                                direct[a][b] = direct[a][b] + straight
                                crossed[a][b] = crossed[a][b] + across
                tiles = []
                for a in range(BLK):
                    joined = []
                    for b in range(BLK):
                        here = jnp.where(low_lane, direct[a][b], crossed[a][b])
                        there = jnp.where(low_lane, crossed[a][b], direct[a][b])
                        joined.append(here + sign_weight * pltpu.roll(there, HALF, 1))
                    for b in range(0, BLK, 2):
                        keep = jnp.where(low_sub, joined[b], joined[b + 1])
                        move = jnp.where(low_sub, joined[b + 1], joined[b])
                        summed = keep + pltpu.roll(move, 4, 0)
                        tiles.append(summed * weight if chunk == 0 else summed)
                out[pl.ds(at, BLK * BLK * 4), :] = jnp.concatenate(tiles, axis=0).astype(jnp.bfloat16)

            @pl.when(p >= count)
            def _():
                out[pl.ds(at, BLK * BLK * 4), :] = jnp.zeros((BLK * BLK * 4, LANES), jnp.bfloat16)

            return carry

        lax.fori_loop(0, slots_each, one_slot, 0)


def cross(scalars, pieces, group_count, chunk, slot_count):
    piece_count = len(pieces)
    out_rows = slot_count // group_count * BLK * BLK * 4
    vmem = pl.BlockSpec(memory_space=pltpu.VMEM)
    held_shape = pieces[0].shape if piece_count == 1 else (piece_count,) + pieces[0].shape
    flops = 8 * slot_count * BLK * BLK * HALF * 4 * SEGS
    moved = 2 * math.prod(held_shape) + 2 * out_rows * LANES * group_count
    return pl.pallas_call(
        lambda *refs: cross_kernel(group_count, piece_count, chunk, *refs),
        out_shape=[jax.ShapeDtypeStruct((out_rows, LANES), jnp.bfloat16)] * group_count,
        in_specs=[pl.BlockSpec(memory_space=pltpu.SMEM)] + [pl.BlockSpec(memory_space=pl.ANY)] * piece_count,
        out_specs=[vmem] * group_count,
        scratch_shapes=[
            pltpu.VMEM(held_shape, jnp.bfloat16),
            pltpu.SemaphoreType.DMA((piece_count,)),
        ],
        cost_estimate=pl.CostEstimate(flops=flops, bytes_accessed=moved, transcendentals=0),
        name="cross",
    )(scalars, *pieces)


def inverse_kernel(group_count, me_ref, mat_ref, twist_ref, *refs):
    inputs = refs[: 2 * group_count]
    out_ref, turned_ref = refs[2 * group_count :]
    group = OUTER // group_count
    inner = mat_ref.shape[1] // 2
    me = me_ref[0]
    for d in range(group_count):
        both = jnp.concatenate([inputs[d][...], inputs[group_count + d][...]], axis=1)
        turned = jnp.dot(both, mat_ref[...], preferred_element_type=jnp.float32)
        for part in range(2 * inner // LANES):
            turned_ref[lax.bitwise_xor(me, d), part] = turned[:, part * LANES : (part + 1) * LANES]
    tile = 16

    def lags(step, carry):
        at = step * tile
        for lane in range(0, inner, LANES):
            spectrum = []
            for k in range(OUTER):
                row = pl.ds(at * group + k % group, tile, stride=group)
                re = turned_ref[k // group, lane // LANES, row, :]
                im = turned_ref[k // group, (inner + lane) // LANES, row, :]
                cos = twist_ref[0, k : k + 1, lane : lane + LANES]
                sin = twist_ref[1, k : k + 1, lane : lane + LANES]
                spectrum.append((re * cos - im * sin, re * sin + im * cos))
            half = [(spectrum[0][0], None)]
            for k in range(1, OUTER // 2):
                half.append(plus(spectrum[k], conj(spectrum[OUTER - k])))
            half.append((spectrum[OUTER // 2][0], None))
            half = [(re * 0.5 if 0 < k < OUTER // 2 else re, None if im is None else im * 0.5) for k, (re, im) in enumerate(half)]
            series = real_inverse(OUTER, half)
            for u in range(OUTER):
                out_ref[pl.ds(pl.multiple_of(at, tile), tile), u * inner + lane : u * inner + lane + LANES] = series[u].astype(
                    jnp.bfloat16
                )
        return carry

    lax.fori_loop(0, out_ref.shape[0] // tile, lags, 0)


def inverse(me, inputs, length):
    group_count = len(inputs) // 2
    group = OUTER // group_count
    out_rows = inputs[0].shape[0] // group
    inner = length // OUTER
    matrix, twist = inverse_tables(length)
    vmem = pl.BlockSpec(memory_space=pltpu.VMEM)
    return pl.pallas_call(
        lambda *refs: inverse_kernel(group_count, *refs),
        out_shape=jax.ShapeDtypeStruct((out_rows, length), jnp.bfloat16),
        in_specs=[pl.BlockSpec(memory_space=pltpu.SMEM)] + [vmem] * (2 + len(inputs)),
        out_specs=vmem,
        scratch_shapes=[pltpu.VMEM((group_count, 2 * inner // LANES, out_rows * group, LANES), jnp.float32)],
        name="inverse",
    )(me, matrix, twist, *inputs)


def exchange(parts, count):
    got = [parts[0]]
    for d in range(1, count):
        got.append(lax.ppermute(parts[d], "seg", [(i, i ^ d) for i in range(count)]))
    return got


def gather_pieces(own, sta_count):
    slow = sta_count // 2

    def shifted(value, step):
        return lax.ppermute(
            value, "sta", [(i, (i // 2 + step) % slow * 2 + i % 2) for i in range(sta_count)]
        )

    def other(value):
        return lax.ppermute(value, "sta", [(i, i ^ 1) for i in range(sta_count)])

    near = [own] + [shifted(own, step) for step in range(1, slow)]
    pieces = []
    for value in near:
        pieces += [value, other(value)]
    return pieces


def local(sta_count, seg_count, traces, pair_blocks, pair_counts):
    stations, _, length = traces.shape
    slot_count = pair_blocks.shape[0]
    block_count = stations // BLK
    seg_me = lax.axis_index("seg").astype(jnp.int32)
    sta_me = lax.axis_index("sta").astype(jnp.int32)
    me = seg_me.reshape(1)
    home = pair_blocks[:, 1] // block_count
    by_shift = sta_count <= 16
    if by_shift:
        slow = sta_count // 2
        shift = (sta_me // 2 - home // 2 + slow) % slow
        piece = shift * 2 + (sta_me ^ home) % 2
        own = jnp.int32(0)
    else:
        piece = home
        own = sta_me
    extra = jnp.stack([seg_me, pair_counts[0], own])
    scalars = jnp.stack(
        [
            pair_blocks[:, 0] % block_count,
            piece,
            pair_blocks[:, 1] % block_count,
            jnp.pad(extra, (0, slot_count - 3)),
        ]
    ).astype(jnp.int32)
    whitened = whiten(me, traces, seg_count)
    received = []
    for chunk in range(2):
        mine = jnp.stack(exchange(whitened[chunk], seg_count))
        if by_shift:
            pieces = gather_pieces(mine, sta_count)
        else:
            pieces = [lax.all_gather(mine, "sta", axis=0)]
        received.append(exchange(cross(scalars, pieces, seg_count, chunk, slot_count), seg_count))
    series = inverse(me, received[0] + received[1], length)
    return series.reshape(slot_count // seg_count, BLK, BLK, length)


def solution(mesh):
    sta_count, seg_count = mesh.shape["sta"], mesh.shape["seg"]
    in_specs = (P("sta", "seg", None), P("sta", None), P("sta"))
    out_specs = P(("sta", "seg"), None, None, None)
    return jax.shard_map(
        lambda *args: local(sta_count, seg_count, *args),
        mesh=mesh,
        in_specs=in_specs,
        out_specs=out_specs,
        check_vma=False,
    )
```
